32 devices in a mesh: grp: 2 (over x), aux: 16 (over z, y, core).
Axes of the slice: x: 2, y: 2, z: 4, core: 2. Of those that a mesh axis runs over, the one named last changes fastest.
Arguments:
- three_index: bfloat16 [64, 256, 256], P('aux'), may hold values from -0.375 to 0.375
- relaxed: bfloat16 [512, 256], P('grp'), parts along dimension 0, may hold values from -0.375 to 0.375
- plus_amplitude: bfloat16 [512, 256], P('grp'), parts along dimension 0, may hold values from -0.375 to 0.375
- minus_amplitude: bfloat16 [512, 256], P('grp'), parts along dimension 0, may hold values from -0.375 to 0.375
- ground: bfloat16 [256, 256], replicated, may hold values from -0.375 to 0.375
- integral_grad: bfloat16 [3, 64, 512, 256], P(None, None, 'aux'), may hold values from -0.09375 to 0.09375
- metric_grad: bfloat16 [3, 64, 64], P(None, 'aux'), may hold values from -0.5 to 0.5
- function_atom: int32 [256], replicated, may hold values from 0 to 31, never falling along the last dimension, each value on 1 to 16 neighbouring positions
- aux_center: int32 [64], P('aux'), may hold values from 0 to 31, never falling along the last dimension, each value on 1 to 4 neighbouring positions
- block_list: int32 [512], replicated, may hold values from 0 to 255, as said below
- block_count: int32 [16], replicated, may hold values from 0 to 32, as said below
Outputs:
- gradient: float32 [3, 64], P(None, 'grp'), parts along dimension 1
The draws below stay inside these ranges and needn't reach their ends.
There are 2 independent parts, one for each index of `grp`. The reference program is written for one: setup_inputs(seed, part) draws one part's arguments, and reference() takes and returns one part's arrays. A program takes and returns all parts, laid end to end along the dimension named above; an argument that names none is the same for every part. Nothing has to cross between parts.
Inputs may be any that keep to these rules, and one draw needn't show every extreme that they name: block_count[d] is the number of live slots of owner d; the counts sum to 256, and at least one owner has 32. `block_list`: slot s of owner d is entry d * 32 + s and is live when s < block_count[d]; each tile pair i * 16 + j is held by exactly one live slot; slots that are not live hold arbitrary tile pairs.
All inputs are finite; a program needn't handle non-finite values.
Results may differ from the reference program's by a relative error of at most 0.0032.
Values may be sent and summed in bfloat16 or wider, within the bound.
A program may use at most 64 MiB of HBM per device.

```python
import math
import jax
import jax.numpy as jnp
import numpy as np
from jax import lax

NBW = 256
TILE = 16
NT = 16
NTP = 256
MAXT = 32
SLOTS = 512
NAUX = 64
NATOM = 32


def owner_layout(key):
    key = jax.random.fold_in(key, 7)
    first_key, second_key, third_key, fourth_key = jax.random.split(key, 4)
    owners = SLOTS // MAXT
    slot_ids = jnp.arange(SLOTS, dtype=jnp.int32)
    slot_owner = slot_ids // MAXT
    filled = jax.random.randint(first_key, (), 0, owners)
    scores = jax.random.permutation(second_key, SLOTS).astype(jnp.int32)
    scores = jnp.where(slot_owner == filled, scores - SLOTS, scores)
    ordering = jnp.argsort(scores, stable=True)
    picked = jnp.zeros((SLOTS,), jnp.int32).at[ordering[:NTP]].set(1)
    counts = picked.reshape(owners, MAXT).sum(axis=1).astype(jnp.int32)
    live_slot = slot_ids % MAXT < counts[slot_owner]
    ranking = jnp.cumsum(live_slot.astype(jnp.int32)) - 1
    tile_order = jax.random.permutation(third_key, NTP).astype(jnp.int32)
    padding = jax.random.randint(fourth_key, (SLOTS,), 0, NTP)
    listing = jnp.where(live_slot, tile_order[jnp.clip(ranking, 0, NTP - 1)], padding).astype(jnp.int32)
    return (listing, counts)


def draw_block_list(key, part):
    return owner_layout(key)[0]


def draw_block_count(key, part):
    return owner_layout(key)[1]


def block_scale(own_key, shape, pieces, low, top_value):
    gain, own = 1.0, jax.random.fold_in(own_key, 6)
    for position, parts in pieces:
        heights = jnp.exp(jax.random.uniform(jax.random.fold_in(own, position), (parts,), jnp.float32, low / len(pieces), top_value / len(pieces)))
        gain = gain * jnp.repeat(heights, shape[position] // parts).reshape([-1 if axis == position else 1 for axis in range(len(shape))])
    return gain


def split_up(count, total, bound, slope):
    portions = [(1 << 20) // math.isqrt(grade ** slope) + 1 for grade in range(2, count + 1)]
    spare, given = total - bound - (count - 1), [1] * (count - 1)
    while spare > 0:
        free = [i for i in range(count - 1) if given[i] < bound]
        pool, budget = sum([portions[i] for i in free]), spare
        for i in free:
            extra = min(bound - given[i], max(1, budget * portions[i] // pool), spare)
            given[i] = given[i] + extra
            spare = spare - extra
    return np.array([bound] + given)


def uneven_parts(stream_key, count, total, bound, lean):
    if count == 2:
        one = jax.random.randint(stream_key, (), max(1, total - bound), min(bound, total - 1) + 1)
        return jnp.stack([one, total - one])
    tallies = jnp.asarray(split_up(count, total, bound, lean), jnp.int32)
    pairs = (count - 1) // 2
    source_of, sink = tallies[1:1 + 2 * pairs:2], tallies[2:2 + 2 * pairs:2]
    margin = jnp.minimum(source_of - 1, bound - sink)
    shifted = jax.random.randint(jax.random.fold_in(stream_key, 1), (pairs,), 0, 1 << 20) % (margin + 1)
    tallies = tallies.at[1:1 + 2 * pairs:2].set(source_of - shifted).at[2:2 + 2 * pairs:2].set(sink + shifted)
    return tallies[jax.random.permutation(jax.random.fold_in(stream_key, 2), count)]


def normal_values(rng, shape, scale, reach, pieces=(), kind=jnp.bfloat16):
    factor_of = block_scale(rng, shape, pieces, -0.22, 0.18) if pieces else 1.0
    entries = jax.random.normal(rng, shape, jnp.float32) * scale * factor_of
    return jnp.minimum(jnp.maximum(entries, -reach), reach).astype(kind)


def setup_inputs(seed: int = 0, part: int = 0) -> dict:
    key_of = jax.random.split(jax.random.key(seed), 12)
    part_splits = jax.random.split(jax.random.fold_in(key_of[11], part), 12)
    return {
        "three_index": normal_values(key_of[0], (NAUX, NBW, NBW), NBW ** -0.5, 0.375, ((0, 16),)),
        "relaxed": normal_values(part_splits[1], (NBW, NBW), NBW ** -0.5, 0.375),
        "plus_amplitude": normal_values(part_splits[2], (NBW, NBW), NBW ** -0.5, 0.375),
        "minus_amplitude": normal_values(part_splits[3], (NBW, NBW), NBW ** -0.5, 0.375),
        "ground": normal_values(key_of[4], (NBW, NBW), NBW ** -0.5, 0.375),
        "integral_grad": normal_values(key_of[5], (3, NAUX, SLOTS, TILE * TILE), (NAUX * NBW // 4) ** -0.5, 0.09375, ((2, 16),)),
        "metric_grad": normal_values(key_of[6], (3, NAUX, NAUX), (NAUX * NAUX // NATOM) ** -0.5, 0.5, ((1, 16),)),
        "function_atom": jnp.searchsorted(jnp.cumsum(uneven_parts(key_of[7], NATOM, NBW, 2 * NBW // NATOM, 1)), jnp.arange(NBW), side="right").astype(jnp.int32),
        "aux_center": jnp.searchsorted(jnp.cumsum(uneven_parts(key_of[8], NATOM, NAUX, 2 * NAUX // NATOM, 1)), jnp.arange(NAUX), side="right").astype(jnp.int32),
        "block_list": draw_block_list(jax.random.fold_in(key_of[11], 71), part),
        "block_count": draw_block_count(jax.random.fold_in(key_of[11], 71), part),
    }


def reference(three_index, relaxed, plus_amplitude, minus_amplitude, ground, integral_grad, metric_grad, function_atom, aux_center, block_list, block_count):
    highest = lax.Precision.HIGHEST
    fitted = jnp.einsum('pab,ab->p', three_index.astype(jnp.float32), relaxed.astype(jnp.float32), precision=highest)
    stacked = jnp.concatenate([plus_amplitude, minus_amplitude, ground], 0)
    relaxed_wide = relaxed.astype(jnp.float32)

    def density_tiles(operands):
        slab, weight = operands
        halves = jnp.dot(stacked, slab, preferred_element_type=jnp.float32).astype(jnp.bfloat16)
        plus_half = halves[:NBW]
        minus_half = halves[NBW:2 * NBW]
        ground_half = halves[2 * NBW:]
        exchange_part = jnp.dot(plus_half, plus_amplitude.T, preferred_element_type=jnp.float32) - jnp.dot(minus_half, minus_amplitude.T, preferred_element_type=jnp.float32)
        crossed = jnp.dot(ground_half, relaxed, preferred_element_type=jnp.float32)
        triple = (weight * relaxed_wide + exchange_part + crossed + crossed.T).astype(jnp.bfloat16)
        return triple.reshape(NT, TILE, NT, TILE).transpose(0, 2, 1, 3).reshape(NTP, TILE * TILE)

    blocked = lax.map(density_tiles, (three_index, fitted))
    chosen = jnp.take(blocked, block_list, axis=1)
    slot_ids = jnp.arange(SLOTS, dtype=jnp.int32)
    live_mask = ((slot_ids % MAXT) < block_count[slot_ids // MAXT]).astype(jnp.float32)

    def contract(component):
        return jnp.sum(chosen.astype(jnp.float32) * component.astype(jnp.float32), axis=0)

    contracted = lax.map(contract, integral_grad)
    row_sums = contracted.reshape(3, SLOTS, TILE, TILE).sum(axis=3) * live_mask[None, :, None]
    function_ids = (block_list // NT)[:, None] * TILE + jnp.arange(TILE, dtype=jnp.int32)[None, :]
    atom_table = (function_atom[function_ids][:, :, None] == jnp.arange(NATOM, dtype=jnp.int32)[None, None, :]).astype(jnp.float32)
    three_part = 2.0 * jnp.einsum('kgm,gma->ka', row_sums, atom_table, precision=highest)
    coupling = jnp.einsum('kpq,q->kp', metric_grad.astype(jnp.float32), fitted, precision=highest)
    aux_table = (aux_center[:, None] == jnp.arange(NATOM, dtype=jnp.int32)[None, :]).astype(jnp.float32)
    metric_part = jnp.einsum('kp,pa->ka', coupling * fitted[None, :], aux_table, precision=highest)
    return three_part - metric_part
```

```python
import functools

import jax
import jax.numpy as jnp
from jax import lax
from jax.experimental import pallas as pl
from jax.experimental.pallas import tpu as pltpu
from jax.sharding import PartitionSpec as P

TILE = 16
NATOM = 32
F32 = jnp.float32
BF16 = jnp.bfloat16
MESH = pl.DeviceIdType.MESH


def iota(shape, axis):
    return lax.broadcasted_iota(jnp.int32, shape, axis)


def dot(a, b, ca=1, cb=0):
    return lax.dot_general(a, b, (((ca,), (cb,)), ((), ())), preferred_element_type=F32)


def swap_tiles(x):
    quads = x.reshape(TILE, 2, 8, 256)
    rows = []
    for high_v in range(2):
        lanes = []
        for high_i in range(2):
            z = quads[:, high_i, :, high_v * 128 : high_v * 128 + 128]
            z = z.reshape(TILE * 8, 128)
            sub = iota(z.shape, 0)
            lane = iota(z.shape, 1) // TILE
            for s in (4, 2, 1):
                bit_i = (sub // s) % 2
                bit_v = (lane // s) % 2
                down = pltpu.roll(z, z.shape[0] - s, 0)
                down = pltpu.roll(down, TILE * s, 1)
                up = pltpu.roll(z, s, 0)
                up = pltpu.roll(up, 128 - TILE * s, 1)
                z = jnp.where(bit_i == bit_v, z, jnp.where(bit_i == 0, down, up))
            lanes.append(z.reshape(TILE, 1, 8, 128))
        rows.append(jnp.concatenate(lanes, axis=3))
    return jnp.concatenate(rows, axis=1).reshape(256, 256)


def density_kernel(
    owners, b_ref, relaxed_ref, plus_ref, minus_ref, ground_ref, list_ref, chosen_ref, fit_ref
):
    aux_local = b_ref.shape[0]
    slots = list_ref.shape[0]
    me = lax.axis_index("aux")
    relaxed = relaxed_ref[...]
    a = iota((256, 256), 0)
    b = iota((256, 256), 1)
    perm = ((a % TILE) * TILE + a // TILE == b).astype(BF16)
    plus = dot(perm, plus_ref[...]).astype(BF16)
    minus = dot(perm, minus_ref[...]).astype(BF16)
    ground = dot(perm, ground_ref[...]).astype(BF16)
    relaxed_cols = dot(relaxed, perm, 1, 1).astype(BF16)
    relaxed_turned = dot(perm, relaxed, 1, 1).astype(BF16)
    relaxed_both = dot(perm, relaxed_cols)
    picked = (list_ref[...] == iota((slots, 256), 1)).astype(BF16)
    lane = iota(fit_ref.shape, 1)
    fit_row = jnp.zeros(fit_ref.shape, F32)
    for p in range(aux_local):
        slab = b_ref[p]
        fitted = jnp.sum(slab.astype(F32) * relaxed.astype(F32), axis=0, keepdims=True)
        fitted = jnp.sum(fitted, axis=1, keepdims=True)
        fit_row = jnp.where(lane == me * aux_local + p, fitted, fit_row)
        plus_half = dot(plus, slab).astype(BF16)
        minus_half = dot(minus, slab).astype(BF16)
        ground_half = dot(ground, slab).astype(BF16)
        triple = (
            fitted * relaxed_both
            + dot(plus_half, plus, 1, 1)
            - dot(minus_half, minus, 1, 1)
            + dot(ground_half, relaxed_cols)
            + dot(relaxed_turned, ground_half, 1, 1)
        )
        blocked = swap_tiles(triple.astype(BF16).astype(F32)).astype(BF16)
        chosen = dot(picked, blocked, 1, 1)
        chosen_ref[:, p] = chosen.reshape(owners, slots // owners, 256).astype(BF16)
    fit_ref[...] = fit_row


def exchange_kernel(
    n,
    count_ref,
    center_ref,
    chosen_ref,
    fit_ref,
    metric_ref,
    list_ref,
    atom_ref,
    integral_ref,
    out_ref,
    integral,
    arrived,
    fits,
    parts,
    load_sems,
    send_sems,
    recv_sems,
    fit_send,
    fit_recv,
    part_send,
    part_recv,
):
    me = lax.axis_index("aux")
    depth = integral.shape[2]
    aux_local = arrived.shape[1]

    loads = [
        pltpu.make_async_copy(integral_ref.at[c], integral.at[c], load_sems.at[c]) for c in range(3)
    ]
    loads.append(pltpu.make_async_copy(chosen_ref.at[me], arrived.at[me], load_sems.at[3]))
    loads.append(pltpu.make_async_copy(fit_ref, fits.at[me], load_sems.at[4]))
    for load in loads:
        load.start()

    barrier = pltpu.get_barrier_semaphore()

    def peer_of(k):
        return lax.rem(me + k, n)

    def greet(k, c):
        pl.semaphore_signal(barrier, inc=1, device_id={"aux": peer_of(k)}, device_id_type=MESH)
        return c

    lax.fori_loop(1, n, greet, 0)
    pl.semaphore_wait(barrier, n - 1)

    def tiles_to(peer, slot):
        return pltpu.make_async_remote_copy(
            src_ref=chosen_ref.at[peer],
            dst_ref=arrived.at[slot],
            send_sem=send_sems.at[peer],
            recv_sem=recv_sems.at[slot],
            device_id={"aux": peer},
            device_id_type=MESH,
        )

    def fit_to(peer, slot):
        return pltpu.make_async_remote_copy(
            src_ref=fit_ref,
            dst_ref=fits.at[slot],
            send_sem=fit_send.at[peer],
            recv_sem=fit_recv.at[slot],
            device_id={"aux": peer},
            device_id_type=MESH,
        )

    def part_to(peer, slot):
        return pltpu.make_async_remote_copy(
            src_ref=parts.at[me],
            dst_ref=parts.at[slot],
            send_sem=part_send.at[peer],
            recv_sem=part_recv.at[slot],
            device_id={"aux": peer},
            device_id_type=MESH,
        )

    def launch(k, c):
        fit_to(peer_of(k), me).start()
        tiles_to(peer_of(k), me).start()
        return c

    lax.fori_loop(1, n, launch, 0)

    a = iota((TILE, 256), 0)
    b = iota((TILE, 256), 1)
    atoms = jnp.where(b // TILE == a, atom_ref[...].astype(F32), 0.0).astype(BF16)
    spread = (iota((256, 256), 0) % TILE == iota((256, 256), 1) // TILE).astype(BF16)
    atoms = dot(atoms, spread).astype(BF16)
    own_list = list_ref[pl.ds(me * depth, depth), :]
    in_row = (own_list // TILE == iota((depth, TILE), 1)).astype(BF16)
    slot_atoms = dot(in_row, atoms)
    live = iota((depth, 256), 0) < count_ref[me]
    slot_atoms = jnp.where(live, slot_atoms, -1.0).astype(jnp.int32)

    for load in loads:
        load.wait()

    def take(src, sums):
        for p in range(aux_local):
            tile = arrived[src, p].astype(F32)
            row = src * aux_local + p
            sums = tuple(
                total + tile * integral[c, row].astype(F32) for c, total in enumerate(sums)
            )
        return sums

    sums = take(me, tuple(jnp.zeros((depth, 256), F32) for _ in range(3)))
    all_fits = fits[me]

    def arrive(k, carry):
        sums, total_fits = carry
        src = lax.rem(me + n - k, n)
        fit_to(src, src).wait_recv()
        total_fits = total_fits + fits[src]
        tiles_to(src, src).wait_recv()
        return take(src, sums), total_fits

    own_fits = all_fits
    sums, all_fits = lax.fori_loop(1, n, arrive, (sums, all_fits))

    lane = iota((1, 128), 1)
    rows = iota((aux_local, all_fits.shape[1]), 0)
    lanes = iota((aux_local, all_fits.shape[1]), 1)
    fit_column = jnp.sum(
        jnp.where(lanes == me * aux_local + rows, own_fits[:1], 0.0), axis=1, keepdims=True
    )
    table = jnp.zeros((aux_local, 128), F32)
    for p in range(aux_local):
        hit = (iota((aux_local, 128), 0) == p) & (iota((aux_local, 128), 1) == center_ref[p])
        table = jnp.where(hit, fit_column, table)
    width = metric_ref.shape[2]
    out_rows = []
    for c in range(3):
        coupling = jnp.sum(
            metric_ref[c].astype(F32) * all_fits[:1, :width], axis=1, keepdims=True
        )
        metric_part = jnp.sum(coupling * table, axis=0, keepdims=True)
        row = -metric_part
        for atom in range(NATOM):
            hit = jnp.where(slot_atoms == atom, sums[c], 0.0)
            hit = jnp.sum(hit, axis=0, keepdims=True)
            hit = jnp.sum(hit, axis=1, keepdims=True)
            row = row + jnp.where(lane == atom, 2.0 * hit, 0.0)
        out_rows.append(row)
    mine = jnp.concatenate(out_rows + [jnp.zeros((5, 128), F32)], axis=0)
    parts[me] = mine

    def send_part(k, c):
        part_to(peer_of(k), me).start()
        return c

    lax.fori_loop(1, n, send_part, 0)

    def take_part(k, total):
        src = lax.rem(me + n - k, n)
        part_to(src, src).wait_recv()
        return total

    lax.fori_loop(1, n, take_part, 0)
    total = jnp.sum(parts[...], axis=0)
    out_ref[...] = total[:3, :NATOM]

    def drain(k, c):
        peer = peer_of(k)
        fit_to(peer, me).wait_send()
        tiles_to(peer, me).wait_send()
        part_to(peer, me).wait_send()
        return c

    lax.fori_loop(1, n, drain, 0)


def on_device(
    n,
    three_index,
    relaxed,
    plus_amplitude,
    minus_amplitude,
    ground,
    integral_grad,
    metric_grad,
    function_atom,
    aux_center,
    block_list,
    block_count,
):
    aux_local = three_index.shape[0]
    slots = block_list.shape[0]
    aux_total, depth, width = integral_grad.shape[1:]
    fit_lanes = -(-aux_total // 128) * 128
    column = block_list.reshape(slots, 1)
    vmem = pl.BlockSpec(memory_space=pltpu.VMEM)
    smem = pl.BlockSpec(memory_space=pltpu.SMEM)
    anywhere = pl.BlockSpec(memory_space=pl.ANY)
    chosen, fit = pl.pallas_call(
        functools.partial(density_kernel, n),
        out_shape=(
            jax.ShapeDtypeStruct((n, aux_local, depth, width), BF16),
            jax.ShapeDtypeStruct((8, fit_lanes), F32),
        ),
        in_specs=[vmem] * 6,
        out_specs=(vmem, vmem),
        name="density",
    )(three_index, relaxed, plus_amplitude, minus_amplitude, ground, column)
    return pl.pallas_call(
        functools.partial(exchange_kernel, n),
        out_shape=jax.ShapeDtypeStruct((3, NATOM), F32),
        in_specs=[smem, smem, anywhere, anywhere, vmem, vmem, vmem, anywhere],
        out_specs=vmem,
        scratch_shapes=[
            pltpu.VMEM((3, aux_total, depth, width), BF16),
            pltpu.VMEM((n, aux_local, depth, width), BF16),
            pltpu.VMEM((n, 8, fit_lanes), F32),
            pltpu.VMEM((n, 8, 128), F32),
            pltpu.SemaphoreType.DMA((5,)),
            pltpu.SemaphoreType.DMA((n,)),
            pltpu.SemaphoreType.DMA((n,)),
            pltpu.SemaphoreType.DMA((n,)),
            pltpu.SemaphoreType.DMA((n,)),
            pltpu.SemaphoreType.DMA((n,)),
            pltpu.SemaphoreType.DMA((n,)),
        ],
        compiler_params=pltpu.CompilerParams(collective_id=0, has_side_effects=True),
        name="exchange",
    )(
        block_count,
        aux_center,
        chosen,
        fit,
        metric_grad,
        column,
        function_atom.reshape(1, -1),
        integral_grad,
    )


def solution(mesh):
    in_specs = (
        P("aux", None, None),
        P("grp", None),
        P("grp", None),
        P("grp", None),
        P(),
        P(None, None, "aux", None),
        P(None, "aux", None),
        P(),
        P("aux"),
        P(),
        P(),
    )
    out_specs = P(None, "grp")
    return jax.shard_map(
        functools.partial(on_device, mesh.shape["aux"]),
        mesh=mesh,
        in_specs=in_specs,
        out_specs=out_specs,
        check_vma=False,
    )
```

```python
import functools

import jax
import jax.numpy as jnp
from jax import lax
from jax.experimental import pallas as pl
from jax.experimental.pallas import tpu as pltpu
from jax.sharding import PartitionSpec as P

TILE = 16
NATOM = 32
F32 = jnp.float32
BF16 = jnp.bfloat16
MESH = pl.DeviceIdType.MESH


def iota(shape, axis):
    return lax.broadcasted_iota(jnp.int32, shape, axis)


def dot(a, b, ca=1, cb=0):
    return lax.dot_general(a, b, (((ca,), (cb,)), ((), ())), preferred_element_type=F32)


def swap_tiles(x):
    quads = x.reshape(TILE, 2, 8, 256)
    rows = []
    for high_v in range(2):
        lanes = []
        for high_i in range(2):
            z = quads[:, high_i, :, high_v * 128 : high_v * 128 + 128]
            z = z.reshape(TILE * 8, 128)
            sub = iota(z.shape, 0)
            lane = iota(z.shape, 1) // TILE
            for s in (4, 2, 1):
                bit_i = (sub // s) % 2
                bit_v = (lane // s) % 2
                down = pltpu.roll(z, z.shape[0] - s, 0)
                down = pltpu.roll(down, TILE * s, 1)
                up = pltpu.roll(z, s, 0)
                up = pltpu.roll(up, 128 - TILE * s, 1)
                z = jnp.where(bit_i == bit_v, z, jnp.where(bit_i == 0, down, up))
            lanes.append(z.reshape(TILE, 1, 8, 128))
        rows.append(jnp.concatenate(lanes, axis=3))
    return jnp.concatenate(rows, axis=1).reshape(256, 256)


def split3(x):
    high = x.astype(BF16)
    rest = x - high.astype(F32)
    middle = rest.astype(BF16)
    low = (rest - middle.astype(F32)).astype(BF16)
    return high, middle, low


def select_dot(x, table):
    rows = x.shape[0]
    terms = dot(jnp.concatenate([t.astype(F32) for t in split3(x)], axis=0).astype(BF16), table)
    return terms[:rows] + terms[rows : 2 * rows] + terms[2 * rows :]


def gradient_kernel(
    n,
    groups,
    count_ref,
    center_ref,
    b_ref,
    relaxed_ref,
    plus_ref,
    minus_ref,
    ground_ref,
    metric_ref,
    list_ref,
    atom_ref,
    integral_ref,
    out_ref,
    integral,
    foreign,
    chosen,
    arrived,
    fits,
    parts,
    load_sems,
    far_send,
    far_recv,
    near_send,
    near_recv,
    send_sems,
    recv_sems,
    fit_send,
    fit_recv,
    part_send,
    part_recv,
):
    me = lax.axis_index("aux")
    group = lax.axis_index("grp")
    half = n // 2
    depth = integral.shape[2]
    aux_local = b_ref.shape[0]
    share = aux_local // groups
    slots = list_ref.shape[1]
    side = me // half
    spot = me % half
    base = side * half
    other_base = (1 - side) * half
    counterpart = other_base + spot

    loads = [
        pltpu.make_async_copy(integral_ref.at[c], integral.at[c], load_sems.at[c]) for c in range(3)
    ]
    for load in loads:
        load.start()

    barrier = pltpu.get_barrier_semaphore()

    def xor(a, k):
        value, bit = me - me, 1
        while bit < n:
            value = value + ((a // bit) % 2 + (k // bit) % 2) % 2 * bit
            bit *= 2
        return value

    def greet(k, c):
        pl.semaphore_signal(barrier, inc=1, device_id={"aux": xor(me, k)}, device_id_type=MESH)
        return c

    lax.fori_loop(1, n, greet, 0)
    for d in range(1, groups):
        pl.semaphore_signal(
            barrier, inc=1, device_id={"grp": lax.rem(group + d, groups)}, device_id_type=MESH
        )

    def far(q):
        p = group * share + q
        return pltpu.make_async_remote_copy(
            src_ref=b_ref.at[p],
            dst_ref=foreign.at[p],
            send_sem=far_send.at[q],
            recv_sem=far_recv.at[q],
            device_id={"aux": counterpart},
            device_id_type=MESH,
        )

    def near(d, q, source):
        p = source * share + q
        return pltpu.make_async_remote_copy(
            src_ref=foreign.at[p],
            dst_ref=foreign.at[p],
            send_sem=near_send.at[d - 1, q],
            recv_sem=near_recv.at[d - 1, q],
            device_id={"grp": lax.rem(group + d, groups)},
            device_id_type=MESH,
        )

    def tiles(p, peer, slot):
        return pltpu.make_async_remote_copy(
            src_ref=chosen.at[peer, p],
            dst_ref=arrived.at[slot, p],
            send_sem=send_sems.at[p, peer],
            recv_sem=recv_sems.at[p, slot],
            device_id={"aux": base + peer},
            device_id_type=MESH,
        )

    def fit_to(peer, slot):
        return pltpu.make_async_remote_copy(
            src_ref=fits.at[spot],
            dst_ref=fits.at[slot],
            send_sem=fit_send.at[peer],
            recv_sem=fit_recv.at[slot],
            device_id={"aux": base + peer},
            device_id_type=MESH,
        )

    def part_to(peer, slot):
        return pltpu.make_async_remote_copy(
            src_ref=parts.at[me],
            dst_ref=parts.at[slot],
            send_sem=part_send.at[peer],
            recv_sem=part_recv.at[slot],
            device_id={"aux": peer},
            device_id_type=MESH,
        )

    pl.semaphore_wait(barrier, n - 1 + groups - 1)
    for q in range(share):
        far(q).start()

    relaxed = relaxed_ref[...]
    a = iota((256, 256), 0)
    b = iota((256, 256), 1)
    perm = ((a % TILE) * TILE + a // TILE == b).astype(BF16)
    plus = dot(perm, plus_ref[...]).astype(BF16)
    minus = dot(perm, minus_ref[...]).astype(BF16)
    ground = dot(perm, ground_ref[...]).astype(BF16)
    relaxed_cols = dot(relaxed, perm, 1, 1).astype(BF16)
    relaxed_turned = dot(perm, relaxed, 1, 1).astype(BF16)
    relaxed_both = dot(perm, relaxed_cols)
    relaxed_wide = relaxed.astype(F32)
    half_slots = slots // 2
    listed = list_ref[...]
    listed = jnp.where(side == 0, listed[:, :half_slots], listed[:, half_slots:])
    picked = (listed == iota((256, half_slots), 0)).astype(F32).T.astype(BF16)
    fit_lane = iota(fits.shape[1:], 1)

    def density(slab, p, owner, fit_row):
        fitted = jnp.sum(slab.astype(F32) * relaxed_wide, axis=0, keepdims=True)
        fitted = jnp.sum(fitted, axis=1, keepdims=True)
        plus_half = dot(plus, slab).astype(BF16)
        minus_half = dot(minus, slab).astype(BF16)
        ground_half = dot(ground, slab).astype(BF16)
        triple = (
            fitted * relaxed_both
            + dot(plus_half, plus, 1, 1)
            - dot(minus_half, minus, 1, 1)
            + dot(ground_half, relaxed_cols)
            + dot(relaxed_turned, ground_half, 1, 1)
        )
        blocked = swap_tiles(triple.astype(BF16).astype(F32)).astype(BF16)
        tile_rows = dot(picked, blocked, 1, 1)
        chosen[:, p] = tile_rows.reshape(half, depth, 256).astype(BF16)

        def send(k, c):
            peer = xor(spot, half - k)
            tiles(p, peer, spot).start()
            return c

        lax.fori_loop(1, half, send, 0)
        return jnp.where(fit_lane == owner, fitted, fit_row)

    def take(p, first, local, sums):
        def add(src, ref, sums):
            tile = ref[src, p].astype(F32)
            row = (first + src) * aux_local + local
            return tuple(
                total + tile * integral[c, row].astype(F32) for c, total in enumerate(sums)
            )

        def arrive(k, sums):
            src = xor(spot, k)
            tiles(p, src, src).wait_recv()
            return add(src, arrived, sums)

        return lax.fori_loop(1, half, arrive, add(spot, chosen, sums))

    fit_row = jnp.zeros(fits.shape[1:], F32)
    for p in range(aux_local):
        fit_row = density(b_ref[p], p, me * aux_local + p, fit_row)

    fa = atom_ref[...]
    atom_table = (iota((128, 256), 0) == fa).astype(F32).T.astype(BF16)
    spread = (iota((256, 256), 0) // TILE == iota((256, 256), 1) % TILE).astype(BF16)
    own = jnp.zeros((depth, 1), jnp.int32)
    wide_list = list_ref[...]
    own_lane = iota((depth, slots), 1) == me * depth + iota((depth, slots), 0)
    own = jnp.sum(jnp.where(own_lane, wide_list.astype(F32), 0.0), axis=1, keepdims=True)
    own = own.astype(jnp.int32)
    live = iota((depth, 256), 0) < count_ref[me]
    row_mask = live & (own // TILE == iota((depth, 256), 1) // TILE)

    for load in loads:
        load.wait()

    sums = tuple(jnp.zeros((depth, 256), F32) for _ in range(3))
    order = [(d, q) for q in range(share) for d in range(groups)]
    for place, (d, q) in enumerate(order):
        source = lax.rem(group + groups - d, groups)
        if d == 0:
            far(q).wait_recv()
            for e in range(1, groups):
                near(e, q, group).start()
        else:
            near(d, q, source).wait_recv()
        p = source * share + q
        fit_row = density(
            foreign[p], aux_local + p, counterpart * aux_local + p, fit_row
        )
        if place == aux_local - 2:
            for own_p in range(aux_local):
                sums = take(own_p, base, own_p, sums)
    fits[spot] = fit_row

    def send_fit(k, c):
        fit_to(xor(spot, half - k), spot).start()
        return c

    lax.fori_loop(1, half, send_fit, 0)
    for d, q in order:
        source = lax.rem(group + groups - d, groups)
        p = source * share + q
        sums = take(aux_local + p, other_base, p, sums)

    def arrive_fit(k, total):
        src = xor(spot, k)
        fit_to(src, src).wait_recv()
        return total + fits[src]

    all_fits = lax.fori_loop(1, half, arrive_fit, fit_row)

    rows = iota((aux_local, all_fits.shape[1]), 0)
    lanes = iota((aux_local, all_fits.shape[1]), 1)
    fit_column = jnp.sum(
        jnp.where(lanes == me * aux_local + rows, fit_row, 0.0), axis=1, keepdims=True
    )
    width = metric_ref.shape[2]
    mine = jnp.zeros((1, 128), F32)
    weighted = []
    for c in range(3):
        coupling = jnp.sum(metric_ref[c].astype(F32) * all_fits[:, :width], axis=1, keepdims=True)
        weighted.append(coupling * fit_column)
    for p in range(aux_local):
        for c in range(3):
            hit = iota((1, 128), 1) == center_ref[p] + c * NATOM
            mine = mine - jnp.where(hit, weighted[c][p : p + 1], 0.0)

    by_function = select_dot(jnp.concatenate(sums, axis=0), spread)
    by_function = [
        jnp.sum(
            jnp.where(row_mask, by_function[c * depth : (c + 1) * depth], 0.0),
            axis=0,
            keepdims=True,
        )
        for c in range(3)
    ]
    by_function = jnp.concatenate(by_function + [jnp.zeros((5, 256), F32)], axis=0)
    by_atom = 2.0 * select_dot(by_function, atom_table)
    lane = iota((1, 128), 1)
    for c in range(3):
        row = by_atom[c : c + 1]
        if c:
            row = pltpu.roll(by_atom, c * NATOM, 1)[c : c + 1]
        mine = mine + jnp.where(lane // NATOM == c, row, 0.0)
    parts[me] = mine

    def send_part(k, c):
        part_to(xor(me, n - k), me).start()
        return c

    lax.fori_loop(1, n, send_part, 0)

    def drain(k, c):
        peer = xor(spot, k)
        fit_to(peer, spot).wait_send()
        for p in range(2 * aux_local):
            tiles(p, peer, spot).wait_send()
        return c

    lax.fori_loop(1, half, drain, 0)
    for q in range(share):
        far(q).wait_send()
        for e in range(1, groups):
            near(e, q, group).wait_send()

    def take_part(k, total):
        src = xor(me, k)
        part_to(src, src).wait_recv()
        return total

    lax.fori_loop(1, n, take_part, 0)
    total = jnp.sum(parts[...], axis=0)
    for c in range(3):
        out_ref[c : c + 1] = total[:, c * NATOM : (c + 1) * NATOM]

    def drain_parts(k, c):
        part_to(xor(me, k), me).wait_send()
        return c

    lax.fori_loop(1, n, drain_parts, 0)


def on_device(
    n,
    groups,
    three_index,
    relaxed,
    plus_amplitude,
    minus_amplitude,
    ground,
    integral_grad,
    metric_grad,
    function_atom,
    aux_center,
    block_list,
    block_count,
):
    aux_local = three_index.shape[0]
    aux_total, depth, width = integral_grad.shape[1:]
    fit_lanes = -(-aux_total // 128) * 128
    half = n // 2
    share = aux_local // groups
    vmem = pl.BlockSpec(memory_space=pltpu.VMEM)
    smem = pl.BlockSpec(memory_space=pltpu.SMEM)
    anywhere = pl.BlockSpec(memory_space=pl.ANY)
    dma = pltpu.SemaphoreType.DMA
    return pl.pallas_call(
        functools.partial(gradient_kernel, n, groups),
        out_shape=jax.ShapeDtypeStruct((3, NATOM), F32),
        in_specs=[smem, smem] + [vmem] * 8 + [anywhere],
        out_specs=vmem,
        scratch_shapes=[
            pltpu.VMEM((3, aux_total, depth, width), BF16),
            pltpu.VMEM(three_index.shape, BF16),
            pltpu.VMEM((half, 2 * aux_local, depth, width), BF16),
            pltpu.VMEM((half, 2 * aux_local, depth, width), BF16),
            pltpu.VMEM((half, 1, fit_lanes), F32),
            pltpu.VMEM((n, 1, 128), F32),
            dma((3,)),
            dma((share,)),
            dma((share,)),
            dma((max(groups - 1, 1), share)),
            dma((max(groups - 1, 1), share)),
            dma((2 * aux_local, half)),
            dma((2 * aux_local, half)),
            dma((half,)),
            dma((half,)),
            dma((n,)),
            dma((n,)),
        ],
        compiler_params=pltpu.CompilerParams(collective_id=0, has_side_effects=True),
        name="gradient",
    )(
        block_count,
        aux_center,
        three_index,
        relaxed,
        plus_amplitude,
        minus_amplitude,
        ground,
        metric_grad,
        block_list.reshape(1, -1),
        function_atom.reshape(1, -1),
        integral_grad,
    )


def solution(mesh):
    in_specs = (
        P("aux", None, None),
        P("grp", None),
        P("grp", None),
        P("grp", None),
        P(),
        P(None, None, "aux", None),
        P(None, "aux", None),
        P(),
        P("aux"),
        P(),
        P(),
    )
    out_specs = P(None, "grp")
    return jax.shard_map(
        functools.partial(on_device, mesh.shape["aux"], mesh.shape["grp"]),
        mesh=mesh,
        in_specs=in_specs,
        out_specs=out_specs,
        check_vma=False,
    )
```

```python
import functools

import jax
import jax.numpy as jnp
from jax import lax
from jax.experimental import pallas as pl
from jax.experimental.pallas import tpu as pltpu
from jax.sharding import PartitionSpec as P

TILE = 16
NATOM = 32
F32 = jnp.float32
BF16 = jnp.bfloat16
MESH = pl.DeviceIdType.MESH


def iota(shape, axis):
    return lax.broadcasted_iota(jnp.int32, shape, axis)


def dot(a, b, ca=1, cb=0):
    return lax.dot_general(a, b, (((ca,), (cb,)), ((), ())), preferred_element_type=F32)


def swap_tiles(x):
    quads = x.reshape(TILE, 2, 8, 256)
    rows = []
    for high_v in range(2):
        lanes = []
        for high_i in range(2):
            z = quads[:, high_i, :, high_v * 128 : high_v * 128 + 128]
            z = z.reshape(TILE * 8, 128)
            sub = iota(z.shape, 0)
            lane = iota(z.shape, 1) // TILE
            for s in (4, 2, 1):
                bit_i = (sub // s) % 2
                bit_v = (lane // s) % 2
                down = pltpu.roll(z, z.shape[0] - s, 0)
                down = pltpu.roll(down, TILE * s, 1)
                up = pltpu.roll(z, s, 0)
                up = pltpu.roll(up, 128 - TILE * s, 1)
                z = jnp.where(bit_i == bit_v, z, jnp.where(bit_i == 0, down, up))
            lanes.append(z.reshape(TILE, 1, 8, 128))
        rows.append(jnp.concatenate(lanes, axis=3))
    return jnp.concatenate(rows, axis=1).reshape(256, 256)


def split3(x):
    high = x.astype(BF16)
    rest = x - high.astype(F32)
    middle = rest.astype(BF16)
    low = (rest - middle.astype(F32)).astype(BF16)
    return high, middle, low


def select_dot(x, table):
    rows = x.shape[0]
    terms = dot(jnp.concatenate([t.astype(F32) for t in split3(x)], axis=0).astype(BF16), table)
    return terms[:rows] + terms[rows : 2 * rows] + terms[2 * rows :]


def gradient_kernel(
    n,
    groups,
    count_ref,
    center_ref,
    metric_ref,
    list_ref,
    atom_ref,
    slab_ref,
    relaxed_ref,
    plus_ref,
    minus_ref,
    ground_ref,
    integral_ref,
    out_ref,
    integral,
    b_ref,
    mats,
    foreign,
    chosen,
    arrived,
    fits,
    parts,
    load_sems,
    far_send,
    far_recv,
    near_send,
    near_recv,
    send_sems,
    recv_sems,
    fit_send,
    fit_recv,
    part_send,
    part_recv,
):
    me = lax.axis_index("aux")
    group = lax.axis_index("grp")
    half = n // 2
    piece = slab_ref.shape[1] // 2
    depth = integral.shape[2]
    aux_local = b_ref.shape[0]
    share = aux_local // groups
    slots = list_ref.shape[1]
    side = me // half
    spot = me % half
    base = side * half
    other_base = (1 - side) * half
    counterpart = other_base + spot

    barrier = pltpu.get_barrier_semaphore()

    def flips(a):
        bits = [1 << i for i in range(n.bit_length() - 1)]
        return [(bit, bit * (1 - 2 * ((a // bit) % 2))) for bit in bits]

    me_flips, spot_flips = flips(me), flips(spot)

    def xor(a, k):
        value = a
        for bit, change in me_flips if a is me else spot_flips:
            if isinstance(k, int):
                value = value + change if k & bit else value
            else:
                value = value + change * ((k // bit) % 2)
        return value

    def loop(first, last, body, carry):
        if n > 16:
            return lax.fori_loop(first, last, body, carry)
        for k in range(first, last):
            carry = body(k, carry)
        return carry

    def greet(k, c):
        pl.semaphore_signal(barrier, inc=1, device_id={"aux": xor(me, k)}, device_id_type=MESH)
        return c

    loop(1, n, greet, 0)
    for d in range(1, groups):
        pl.semaphore_signal(
            barrier, inc=1, device_id={"grp": lax.rem(group + d, groups)}, device_id_type=MESH
        )

    def far(q, h):
        p = group * share + q
        rows = pl.ds(h * piece, piece)
        return pltpu.make_async_remote_copy(
            src_ref=slab_ref.at[p, rows],
            dst_ref=foreign.at[p, rows],
            send_sem=far_send.at[q, h],
            recv_sem=far_recv.at[q, h],
            device_id={"aux": counterpart},
            device_id_type=MESH,
        )

    def near(d, q, h, source):
        p = source * share + q
        rows = pl.ds(h * piece, piece)
        return pltpu.make_async_remote_copy(
            src_ref=foreign.at[p, rows],
            dst_ref=foreign.at[p, rows],
            send_sem=near_send.at[d - 1, q, h],
            recv_sem=near_recv.at[d - 1, q, h],
            device_id={"grp": lax.rem(group + d, groups)},
            device_id_type=MESH,
        )

    def tiles(p, peer, slot):
        return pltpu.make_async_remote_copy(
            src_ref=chosen.at[peer, p],
            dst_ref=arrived.at[slot, p],
            send_sem=send_sems.at[p, peer],
            recv_sem=recv_sems.at[p, slot],
            device_id={"aux": base + peer},
            device_id_type=MESH,
        )

    def fit_to(peer, slot):
        return pltpu.make_async_remote_copy(
            src_ref=fits.at[spot],
            dst_ref=fits.at[slot],
            send_sem=fit_send.at[peer],
            recv_sem=fit_recv.at[slot],
            device_id={"aux": base + peer},
            device_id_type=MESH,
        )

    def part_to(peer, slot):
        return pltpu.make_async_remote_copy(
            src_ref=parts.at[me],
            dst_ref=parts.at[slot],
            send_sem=part_send.at[peer],
            recv_sem=part_recv.at[slot],
            device_id={"aux": peer},
            device_id_type=MESH,
        )

    loads = [
        pltpu.make_async_copy(ref, mats.at[i], load_sems.at[i])
        for i, ref in enumerate((relaxed_ref, plus_ref, minus_ref, ground_ref))
    ]
    loads.append(pltpu.make_async_copy(slab_ref, b_ref, load_sems.at[4]))
    late = [
        pltpu.make_async_copy(integral_ref.at[c], integral.at[c], load_sems.at[5 + c])
        for c in range(3)
    ]
    for load in loads + late:
        load.start()
    pl.semaphore_wait(barrier, n - 1 + groups - 1)
    for q in range(share):
        for h in range(2):
            far(q, h).start()
    for load in loads:
        load.wait()

    relaxed = mats[0]
    stacked = mats[1:4].reshape(3 * 256, 256)
    relaxed_wide = relaxed.astype(F32)
    turned = relaxed_wide.T.astype(BF16)
    partners = jnp.concatenate(
        [mats[1].astype(F32).T, -(mats[2].astype(F32).T), relaxed_wide], axis=0
    ).astype(BF16)
    half_slots = slots // 2
    listed = list_ref[...]
    listed = jnp.where(side == 0, listed[:, :half_slots], listed[:, half_slots:])
    picked = (listed == iota((256, half_slots), 0)).astype(F32).T.astype(BF16)
    fit_lane = iota(fits.shape[1:], 1)


    def density(slab, p, owner, fit_row):
        fitted = jnp.sum(slab.astype(F32) * relaxed_wide, axis=0, keepdims=True)
        fitted = jnp.sum(fitted, axis=1, keepdims=True)
        halves = dot(stacked, slab).astype(BF16)
        ground_half = halves[512:]
        joined = jnp.concatenate([halves[:256], halves[256:512], ground_half], axis=1)
        triple = (
            fitted * relaxed_wide + dot(joined, partners) + dot(turned, ground_half, 1, 1)
        )
        blocked = swap_tiles(triple.astype(BF16).astype(F32)).astype(BF16)
        tile_rows = dot(picked, blocked)
        chosen[:, p] = tile_rows.reshape(half, depth, 256).astype(BF16)

        def send(k, c):
            peer = xor(spot, half - k)
            tiles(p, peer, spot).start()
            return c

        loop(1, half, send, 0)
        return jnp.where(fit_lane == owner, fitted, fit_row)

    def take(p, first, local, sums):
        def add(src, ref, sums):
            tile = ref[src, p].astype(F32)
            row = (first + src) * aux_local + local
            return tuple(
                total + tile * integral[c, row].astype(F32) for c, total in enumerate(sums)
            )

        def arrive(k, sums):
            src = xor(spot, k)
            tiles(p, src, src).wait_recv()
            return add(src, arrived, sums)

        return loop(1, half, arrive, add(spot, chosen, sums))

    fit_row = jnp.zeros(fits.shape[1:], F32)
    for p in range(aux_local):
        fit_row = density(b_ref[p], p, me * aux_local + p, fit_row)

    fa = atom_ref[...]
    atom_table = (iota((128, 256), 0) == fa).astype(F32).T.astype(BF16)
    spread = (iota((256, 256), 0) // TILE == iota((256, 256), 1) % TILE).astype(BF16)
    own = jnp.zeros((depth, 1), jnp.int32)
    wide_list = list_ref[...]
    own_lane = iota((depth, slots), 1) == me * depth + iota((depth, slots), 0)
    own = jnp.sum(jnp.where(own_lane, wide_list.astype(F32), 0.0), axis=1, keepdims=True)
    own = own.astype(jnp.int32)
    live = iota((depth, 256), 0) < count_ref[me]
    row_mask = live & (own // TILE == iota((depth, 256), 1) // TILE)

    for load in late:
        load.wait()

    sums = tuple(jnp.zeros((depth, 256), F32) for _ in range(3))
    order = [(d, q) for q in range(share) for d in range(groups)]
    for d, q in order:
        source = lax.rem(group + groups - d, groups)
        for h in range(2):
            if d == 0:
                far(q, h).wait_recv()
                for e in range(1, groups):
                    near(e, q, h, group).start()
            else:
                near(d, q, h, source).wait_recv()
        p = source * share + q
        fit_row = density(
            foreign[p], aux_local + p, counterpart * aux_local + p, fit_row
        )
        if (d, q) == (0, share - 1):
            for own_p in range(aux_local):
                sums = take(own_p, base, own_p, sums)
    fits[spot] = fit_row

    def send_fit(k, c):
        fit_to(xor(spot, half - k), spot).start()
        return c

    loop(1, half, send_fit, 0)
    for d, q in order:
        source = lax.rem(group + groups - d, groups)
        p = source * share + q
        sums = take(aux_local + p, other_base, p, sums)

    def arrive_fit(k, total):
        src = xor(spot, k)
        fit_to(src, src).wait_recv()
        return total + fits[src]

    all_fits = loop(1, half, arrive_fit, fit_row)

    rows = iota((aux_local, all_fits.shape[1]), 0)
    lanes = iota((aux_local, all_fits.shape[1]), 1)
    fit_column = jnp.sum(
        jnp.where(lanes == me * aux_local + rows, fit_row, 0.0), axis=1, keepdims=True
    )
    width = metric_ref.shape[2]
    mine = jnp.zeros((1, 128), F32)
    weighted = []
    for c in range(3):
        coupling = jnp.sum(metric_ref[c].astype(F32) * all_fits[:, :width], axis=1, keepdims=True)
        weighted.append(coupling * fit_column)
    for p in range(aux_local):
        for c in range(3):
            hit = iota((1, 128), 1) == center_ref[p] + c * NATOM
            mine = mine - jnp.where(hit, weighted[c][p : p + 1], 0.0)

    by_function = select_dot(jnp.concatenate(sums, axis=0), spread)
    by_function = [
        jnp.sum(
            jnp.where(row_mask, by_function[c * depth : (c + 1) * depth], 0.0),
            axis=0,
            keepdims=True,
        )
        for c in range(3)
    ]
    by_function = jnp.concatenate(by_function + [jnp.zeros((5, 256), F32)], axis=0)
    by_atom = 2.0 * select_dot(by_function, atom_table)
    lane = iota((1, 128), 1)
    for c in range(3):
        row = by_atom[c : c + 1]
        if c:
            row = pltpu.roll(by_atom, c * NATOM, 1)[c : c + 1]
        mine = mine + jnp.where(lane // NATOM == c, row, 0.0)
    parts[me] = mine

    def send_part(k, c):
        part_to(xor(me, n - k), me).start()
        return c

    loop(1, n, send_part, 0)

    def drain(k, c):
        peer = xor(spot, k)
        fit_to(peer, spot).wait_send()
        for p in range(2 * aux_local):
            tiles(p, peer, spot).wait_send()
        return c

    loop(1, half, drain, 0)
    for q in range(share):
        for h in range(2):
            far(q, h).wait_send()
            for e in range(1, groups):
                near(e, q, h, group).wait_send()

    def take_part(k, total):
        src = xor(me, k)
        part_to(src, src).wait_recv()
        return total

    loop(1, n, take_part, 0)
    total = jnp.sum(parts[...], axis=0)
    for c in range(3):
        row = pltpu.roll(jnp.broadcast_to(total, (8, 128)), 128 - c * NATOM, 1) if c else total
        out_ref[c : c + 1] = row[:1]

    def drain_parts(k, c):
        part_to(xor(me, k), me).wait_send()
        return c

    loop(1, n, drain_parts, 0)


def on_device(
    n,
    groups,
    three_index,
    relaxed,
    plus_amplitude,
    minus_amplitude,
    ground,
    integral_grad,
    metric_grad,
    function_atom,
    aux_center,
    block_list,
    block_count,
):
    aux_local = three_index.shape[0]
    aux_total, depth, width = integral_grad.shape[1:]
    fit_lanes = -(-aux_total // 128) * 128
    half = n // 2
    share = aux_local // groups
    vmem = pl.BlockSpec(memory_space=pltpu.VMEM)
    smem = pl.BlockSpec(memory_space=pltpu.SMEM)
    anywhere = pl.BlockSpec(memory_space=pl.ANY)
    dma = pltpu.SemaphoreType.DMA
    out = pl.pallas_call(
        functools.partial(gradient_kernel, n, groups),
        out_shape=jax.ShapeDtypeStruct((3, 128), F32),
        in_specs=[smem, smem] + [vmem] * 3 + [anywhere] * 6,
        out_specs=vmem,
        scratch_shapes=[
            pltpu.VMEM((3, aux_total, depth, width), BF16),
            pltpu.VMEM(three_index.shape, BF16),
            pltpu.VMEM((4, *relaxed.shape), BF16),
            pltpu.VMEM(three_index.shape, BF16),
            pltpu.VMEM((half, 2 * aux_local, depth, width), BF16),
            pltpu.VMEM((half, 2 * aux_local, depth, width), BF16),
            pltpu.VMEM((half, 1, fit_lanes), F32),
            pltpu.VMEM((n, 1, 128), F32),
            dma((8,)),
            dma((share, 2)),
            dma((share, 2)),
            dma((max(groups - 1, 1), share, 2)),
            dma((max(groups - 1, 1), share, 2)),
            dma((2 * aux_local, half)),
            dma((2 * aux_local, half)),
            dma((half,)),
            dma((half,)),
            dma((n,)),
            dma((n,)),
        ],
        compiler_params=pltpu.CompilerParams(collective_id=0, has_side_effects=True),
        name="gradient",
    )(
        block_count,
        aux_center,
        metric_grad,
        block_list.reshape(1, -1),
        function_atom.reshape(1, -1),
        three_index,
        relaxed,
        plus_amplitude,
        minus_amplitude,
        ground,
        integral_grad,
    )
    return out[:, :NATOM]


def solution(mesh):
    in_specs = (
        P("aux", None, None),
        P("grp", None),
        P("grp", None),
        P("grp", None),
        P(),
        P(None, None, "aux", None),
        P(None, "aux", None),
        P(),
        P("aux"),
        P(),
        P(),
    )
    out_specs = P(None, "grp")
    return jax.shard_map(
        functools.partial(on_device, mesh.shape["aux"], mesh.shape["grp"]),
        mesh=mesh,
        in_specs=in_specs,
        out_specs=out_specs,
        check_vma=False,
    )
```

```python
import functools

import jax
import jax.numpy as jnp
from jax import lax
from jax.experimental import pallas as pl
from jax.experimental.pallas import tpu as pltpu
from jax.sharding import PartitionSpec as P

TILE = 16
NATOM = 32
F32 = jnp.float32
BF16 = jnp.bfloat16
MESH = pl.DeviceIdType.MESH


def iota(shape, axis):
    return lax.broadcasted_iota(jnp.int32, shape, axis)


def dot(a, b, ca=1, cb=0):
    return lax.dot_general(a, b, (((ca,), (cb,)), ((), ())), preferred_element_type=F32)


def swap_tiles(x):
    quads = x.reshape(TILE, 2, 8, 256)
    rows = []
    for high_v in range(2):
        lanes = []
        for high_i in range(2):
            z = quads[:, high_i, :, high_v * 128 : high_v * 128 + 128]
            z = z.reshape(TILE * 8, 128)
            sub = iota(z.shape, 0)
            lane = iota(z.shape, 1) // TILE
            for s in (4, 2, 1):
                bit_i = (sub // s) % 2
                bit_v = (lane // s) % 2
                down = pltpu.roll(z, z.shape[0] - s, 0)
                down = pltpu.roll(down, TILE * s, 1)
                up = pltpu.roll(z, s, 0)
                up = pltpu.roll(up, 128 - TILE * s, 1)
                z = jnp.where(bit_i == bit_v, z, jnp.where(bit_i == 0, down, up))
            lanes.append(z.reshape(TILE, 1, 8, 128))
        rows.append(jnp.concatenate(lanes, axis=3))
    return jnp.concatenate(rows, axis=1).reshape(256, 256)


def split3(x):
    high = x.astype(BF16)
    rest = x - high.astype(F32)
    middle = rest.astype(BF16)
    low = (rest - middle.astype(F32)).astype(BF16)
    return high, middle, low


def select_dot(x, table):
    rows = x.shape[0]
    terms = dot(jnp.concatenate([t.astype(F32) for t in split3(x)], axis=0).astype(BF16), table)
    return terms[:rows] + terms[rows : 2 * rows] + terms[2 * rows :]


def gradient_kernel(
    n,
    groups,
    count_ref,
    center_ref,
    metric_ref,
    list_ref,
    atom_ref,
    slab_ref,
    relaxed_ref,
    plus_ref,
    minus_ref,
    ground_ref,
    integral_ref,
    out_ref,
    integral,
    b_ref,
    mats,
    foreign,
    chosen,
    arrived,
    fits,
    parts,
    load_sems,
    far_send,
    far_recv,
    near_send,
    near_recv,
    send_sems,
    recv_sems,
    fit_send,
    fit_recv,
    part_send,
    part_recv,
):
    me = lax.axis_index("aux")
    group = lax.axis_index("grp")
    half = n // 2
    piece = slab_ref.shape[1] // 2
    depth = integral.shape[2]
    aux_local = b_ref.shape[0]
    share = aux_local // groups
    slots = list_ref.shape[1]
    side = me // half
    spot = me % half
    base = side * half
    other_base = (1 - side) * half
    counterpart = other_base + spot

    barrier = pltpu.get_barrier_semaphore()

    def flips(a):
        bits = [1 << i for i in range(n.bit_length() - 1)]
        return [(bit, bit * (1 - 2 * ((a // bit) % 2))) for bit in bits]

    me_flips, spot_flips = flips(me), flips(spot)

    def xor(a, k):
        value = a
        for bit, change in me_flips if a is me else spot_flips:
            if isinstance(k, int):
                value = value + change if k & bit else value
            else:
                value = value + change * ((k // bit) % 2)
        return value

    def loop(first, last, body, carry):
        if n > 16:
            return lax.fori_loop(first, last, body, carry)
        for k in range(first, last):
            carry = body(k, carry)
        return carry

    def greet(k, c):
        pl.semaphore_signal(barrier, inc=1, device_id={"aux": xor(me, k)}, device_id_type=MESH)
        return c

    loop(1, n, greet, 0)
    for d in range(1, groups):
        pl.semaphore_signal(
            barrier, inc=1, device_id={"grp": lax.rem(group + d, groups)}, device_id_type=MESH
        )

    def far(q, h):
        p = group * share + q
        rows = pl.ds(h * piece, piece)
        return pltpu.make_async_remote_copy(
            src_ref=slab_ref.at[p, rows],
            dst_ref=foreign.at[p, rows],
            send_sem=far_send.at[q, h],
            recv_sem=far_recv.at[q, h],
            device_id={"aux": counterpart},
            device_id_type=MESH,
        )

    def near(d, q, h, source):
        p = source * share + q
        rows = pl.ds(h * piece, piece)
        return pltpu.make_async_remote_copy(
            src_ref=foreign.at[p, rows],
            dst_ref=foreign.at[p, rows],
            send_sem=near_send.at[d - 1, q, h],
            recv_sem=near_recv.at[d - 1, q, h],
            device_id={"grp": lax.rem(group + d, groups)},
            device_id_type=MESH,
        )

    def tiles(p, peer, slot):
        return pltpu.make_async_remote_copy(
            src_ref=chosen.at[peer, p],
            dst_ref=arrived.at[slot, p],
            send_sem=send_sems.at[p, peer],
            recv_sem=recv_sems.at[p, slot],
            device_id={"aux": base + peer},
            device_id_type=MESH,
        )

    def fit_to(peer, slot):
        return pltpu.make_async_remote_copy(
            src_ref=fits.at[spot],
            dst_ref=fits.at[slot],
            send_sem=fit_send.at[peer],
            recv_sem=fit_recv.at[slot],
            device_id={"aux": base + peer},
            device_id_type=MESH,
        )

    def part_to(peer, slot):
        return pltpu.make_async_remote_copy(
            src_ref=parts.at[me],
            dst_ref=parts.at[slot],
            send_sem=part_send.at[peer],
            recv_sem=part_recv.at[slot],
            device_id={"aux": peer},
            device_id_type=MESH,
        )

    loads = [
        pltpu.make_async_copy(ref, mats.at[i], load_sems.at[i])
        for i, ref in enumerate((relaxed_ref, plus_ref, minus_ref, ground_ref))
    ]
    loads.append(pltpu.make_async_copy(slab_ref, b_ref, load_sems.at[4]))
    late = [
        pltpu.make_async_copy(integral_ref.at[c], integral.at[c], load_sems.at[5 + c])
        for c in range(3)
    ]
    for load in loads + late:
        load.start()
    pl.semaphore_wait(barrier, n - 1 + groups - 1)
    for q in range(share):
        for h in range(2):
            far(q, h).start()
    for load in loads:
        load.wait()

    relaxed = mats[0]
    stacked = mats[1:4].reshape(3 * 256, 256)
    relaxed_wide = relaxed.astype(F32)
    turned = relaxed_wide.T.astype(BF16)
    partners = jnp.concatenate(
        [mats[1].astype(F32).T, -(mats[2].astype(F32).T), relaxed_wide], axis=0
    ).astype(BF16)
    half_slots = slots // 2
    listed = list_ref[...]
    listed = jnp.where(side == 0, listed[:, :half_slots], listed[:, half_slots:])
    picked = (listed == iota((256, half_slots), 0)).astype(F32).T.astype(BF16)
    fit_lane = iota(fits.shape[1:], 1)


    def density(slab, p, owner, fit_row):
        fitted = jnp.sum(slab.astype(F32) * relaxed_wide, axis=0, keepdims=True)
        fitted = jnp.sum(fitted, axis=1, keepdims=True)
        halves = dot(stacked, slab).astype(BF16)
        ground_half = halves[512:]
        joined = jnp.concatenate([halves[:256], halves[256:512], ground_half], axis=1)
        triple = (
            fitted * relaxed_wide + dot(joined, partners) + dot(turned, ground_half, 1, 1)
        )
        blocked = swap_tiles(triple.astype(BF16).astype(F32)).astype(BF16)
        tile_rows = dot(picked, blocked)
        chosen[:, p] = tile_rows.reshape(half, depth, 256).astype(BF16)

        def send(k, c):
            peer = xor(spot, half - k)
            tiles(p, peer, spot).start()
            return c

        loop(1, half, send, 0)
        return jnp.where(fit_lane == owner, fitted, fit_row)

    def take(p, first, local, sums):
        def add(src, ref, sums):
            tile = ref[src, p].astype(F32)
            row = (first + src) * aux_local + local
            return tuple(
                total + tile * integral[c, row].astype(F32) for c, total in enumerate(sums)
            )

        def arrive(k, sums):
            src = xor(spot, k)
            tiles(p, src, src).wait_recv()
            return add(src, arrived, sums)

        return loop(1, half, arrive, add(spot, chosen, sums))

    def forward(q, h):
        far(q, h).wait_recv()
        for e in range(1, groups):
            near(e, q, h, group).start()

    fit_row = jnp.zeros(fits.shape[1:], F32)
    for p in range(aux_local):
        if p == aux_local - 1:
            forward(0, 0)
        fit_row = density(b_ref[p], p, me * aux_local + p, fit_row)

    fa = atom_ref[...]
    atom_table = (iota((128, 256), 0) == fa).astype(F32).T.astype(BF16)
    spread = (iota((256, 256), 0) // TILE == iota((256, 256), 1) % TILE).astype(BF16)
    own = jnp.zeros((depth, 1), jnp.int32)
    wide_list = list_ref[...]
    own_lane = iota((depth, slots), 1) == me * depth + iota((depth, slots), 0)
    own = jnp.sum(jnp.where(own_lane, wide_list.astype(F32), 0.0), axis=1, keepdims=True)
    own = own.astype(jnp.int32)
    live = iota((depth, 256), 0) < count_ref[me]
    row_mask = live & (own // TILE == iota((depth, 256), 1) // TILE)

    for load in late:
        load.wait()

    sums = tuple(jnp.zeros((depth, 256), F32) for _ in range(3))
    order = [(d, q) for q in range(share) for d in range(groups)]
    for d, q in order:
        source = lax.rem(group + groups - d, groups)
        for h in range(2):
            if d:
                near(d, q, h, source).wait_recv()
            elif q == 0 and h == 1:
                forward(q, h)
        if d == groups - 1 and q + 1 < share:
            for h in range(2):
                forward(q + 1, h)
        p = source * share + q
        fit_row = density(
            foreign[p], aux_local + p, counterpart * aux_local + p, fit_row
        )
        if (d, q) == (0, share - 1):
            for own_p in range(aux_local):
                sums = take(own_p, base, own_p, sums)
    fits[spot] = fit_row

    def send_fit(k, c):
        fit_to(xor(spot, half - k), spot).start()
        return c

    loop(1, half, send_fit, 0)
    for d, q in order:
        source = lax.rem(group + groups - d, groups)
        p = source * share + q
        sums = take(aux_local + p, other_base, p, sums)

    def arrive_fit(k, total):
        src = xor(spot, k)
        fit_to(src, src).wait_recv()
        return total + fits[src]

    all_fits = loop(1, half, arrive_fit, fit_row)

    rows = iota((aux_local, all_fits.shape[1]), 0)
    lanes = iota((aux_local, all_fits.shape[1]), 1)
    fit_column = jnp.sum(
        jnp.where(lanes == me * aux_local + rows, fit_row, 0.0), axis=1, keepdims=True
    )
    width = metric_ref.shape[2]
    mine = jnp.zeros((1, 128), F32)
    weighted = []
    for c in range(3):
        coupling = jnp.sum(metric_ref[c].astype(F32) * all_fits[:, :width], axis=1, keepdims=True)
        weighted.append(coupling * fit_column)
    for p in range(aux_local):
        for c in range(3):
            hit = iota((1, 128), 1) == center_ref[p] + c * NATOM
            mine = mine - jnp.where(hit, weighted[c][p : p + 1], 0.0)

    by_function = select_dot(jnp.concatenate(sums, axis=0), spread)
    by_function = [
        jnp.sum(
            jnp.where(row_mask, by_function[c * depth : (c + 1) * depth], 0.0),
            axis=0,
            keepdims=True,
        )
        for c in range(3)
    ]
    by_function = jnp.concatenate(by_function + [jnp.zeros((5, 256), F32)], axis=0)
    by_atom = 2.0 * select_dot(by_function, atom_table)
    lane = iota((1, 128), 1)
    for c in range(3):
        row = by_atom[c : c + 1]
        if c:
            row = pltpu.roll(by_atom, c * NATOM, 1)[c : c + 1]
        mine = mine + jnp.where(lane // NATOM == c, row, 0.0)
    parts[me] = mine

    def send_part(k, c):
        part_to(xor(me, n - k), me).start()
        return c

    loop(1, n, send_part, 0)

    def drain(k, c):
        peer = xor(spot, k)
        fit_to(peer, spot).wait_send()
        for p in range(2 * aux_local):
            tiles(p, peer, spot).wait_send()
        return c

    loop(1, half, drain, 0)
    for q in range(share):
        for h in range(2):
            far(q, h).wait_send()
            for e in range(1, groups):
                near(e, q, h, group).wait_send()

    def take_part(k, total):
        src = xor(me, k)
        part_to(src, src).wait_recv()
        return total

    loop(1, n, take_part, 0)
    total = jnp.sum(parts[...], axis=0)
    for c in range(3):
        row = pltpu.roll(jnp.broadcast_to(total, (8, 128)), 128 - c * NATOM, 1) if c else total
        out_ref[c : c + 1] = row[:1]

    def drain_parts(k, c):
        part_to(xor(me, k), me).wait_send()
        return c

    loop(1, n, drain_parts, 0)


def on_device(
    n,
    groups,
    three_index,
    relaxed,
    plus_amplitude,
    minus_amplitude,
    ground,
    integral_grad,
    metric_grad,
    function_atom,
    aux_center,
    block_list,
    block_count,
):
    aux_local = three_index.shape[0]
    aux_total, depth, width = integral_grad.shape[1:]
    fit_lanes = -(-aux_total // 128) * 128
    half = n // 2
    share = aux_local // groups
    vmem = pl.BlockSpec(memory_space=pltpu.VMEM)
    smem = pl.BlockSpec(memory_space=pltpu.SMEM)
    anywhere = pl.BlockSpec(memory_space=pl.ANY)
    dma = pltpu.SemaphoreType.DMA
    out = pl.pallas_call(
        functools.partial(gradient_kernel, n, groups),
        out_shape=jax.ShapeDtypeStruct((3, 128), F32),
        in_specs=[smem, smem] + [vmem] * 3 + [anywhere] * 6,
        out_specs=vmem,
        scratch_shapes=[
            pltpu.VMEM((3, aux_total, depth, width), BF16),
            pltpu.VMEM(three_index.shape, BF16),
            pltpu.VMEM((4, *relaxed.shape), BF16),
            pltpu.VMEM(three_index.shape, BF16),
            pltpu.VMEM((half, 2 * aux_local, depth, width), BF16),
            pltpu.VMEM((half, 2 * aux_local, depth, width), BF16),
            pltpu.VMEM((half, 1, fit_lanes), F32),
            pltpu.VMEM((n, 1, 128), F32),
            dma((8,)),
            dma((share, 2)),
            dma((share, 2)),
            dma((max(groups - 1, 1), share, 2)),
            dma((max(groups - 1, 1), share, 2)),
            dma((2 * aux_local, half)),
            dma((2 * aux_local, half)),
            dma((half,)),
            dma((half,)),
            dma((n,)),
            dma((n,)),
        ],
        compiler_params=pltpu.CompilerParams(collective_id=0, has_side_effects=True),
        name="gradient",
    )(
        block_count,
        aux_center,
        metric_grad,
        block_list.reshape(1, -1),
        function_atom.reshape(1, -1),
        three_index,
        relaxed,
        plus_amplitude,
        minus_amplitude,
        ground,
        integral_grad,
    )
    return out[:, :NATOM]


def solution(mesh):
    in_specs = (
        P("aux", None, None),
        P("grp", None),
        P("grp", None),
        P("grp", None),
        P(),
        P(None, None, "aux", None),
        P(None, "aux", None),
        P(),
        P("aux"),
        P(),
        P(),
    )
    out_specs = P(None, "grp")
    return jax.shard_map(
        functools.partial(on_device, mesh.shape["aux"], mesh.shape["grp"]),
        mesh=mesh,
        in_specs=in_specs,
        out_specs=out_specs,
        check_vma=False,
    )
```
